32 devices in a mesh: groups: 2 (over x), blk: 16 (over z, y, core).
Axes of the slice: x: 2, y: 2, z: 4, core: 2. Of those that a mesh axis runs over, the one named last changes fastest.
Arguments:
- tokens: bfloat16 [8192, 8192], P(('groups', 'blk')), parts along dimension 0, may hold values from -6 to 6
- shrink_panels: bfloat16 [32, 8192, 64], P(None, 'blk'), may hold values from -0.0625 to 0.0625
- expand_panels: bfloat16 [32, 64, 8192], P(None, None, 'blk'), may hold values from -0.75 to 0.75
- adapter_scale: float32 [32], replicated, may hold values from 0.5 to 2
- block_adapter: int32 [128, 1], P('groups'), parts along dimension 0, may hold values from 0 to 31
- shard_counts: int32 [32], P('groups'), parts along dimension 0, may hold values from 1 to 256, as said below
Outputs:
- update: bfloat16 [8192, 8192], P(('groups', 'blk')), parts along dimension 0
The draws below stay inside these ranges and needn't reach their ends.
There are 2 independent parts, one for each index of `groups`. The reference program is written for one: setup_inputs(seed, part) draws one part's arguments, and reference() takes and returns one part's arrays. A program takes and returns all parts, laid end to end along the dimension named above; an argument that names none is the same for every part. Nothing has to cross between parts.
Inputs may be any that keep to these rules, and one draw needn't show every extreme that they name: `shard_counts`: every shard holds at least one live row; in every draw some shard is full.
All inputs are finite; a program needn't handle non-finite values.
Results may differ from the reference program's by a relative error of at most 0.0049.
Values may be sent and summed in bfloat16 or wider, within the bound.
A program may use at most 128 MiB of HBM per device.

```python
import math
import jax
import jax.numpy as jnp
from jax import lax

D = 8192
R = 64
BLOCK = 64
TOK_DEV = 256
TOKENS = 4096
NBLOCKS = 64
ADAPTERS = 32
N_BLK = 16


def draw_shard_counts(key, part):
    values = jax.random.randint(key, (N_BLK,), 1, TOK_DEV + 1, dtype=jnp.int32)
    full_shard = jax.random.randint(jax.random.fold_in(key, 7), (), 0, N_BLK, dtype=jnp.int32)
    marker = jnp.arange(N_BLK, dtype=jnp.int32) == full_shard
    return jnp.where(marker, TOK_DEV, values).astype(jnp.int32)


def steps_of(key, extent, shards, least, largest):
    factor_of, own = 1.0, jax.random.fold_in(key, 6)
    for position, parts in shards:
        draws = jnp.exp(jax.random.uniform(jax.random.fold_in(own, position), (parts,), jnp.float32, least / len(shards), largest / len(shards)))
        factor_of = factor_of * jnp.repeat(draws, extent[position] // parts).reshape([-1 if axis == position else 1 for axis in range(len(extent))])
    return factor_of


def picks_of(key, rows, number_of, top, lift):
    ranking = jax.random.permutation(jax.random.fold_in(key, 1), number_of)
    favour = ranking
    for power in range(3):
        favour = favour * favour // number_of
    favour = favour * lift // number_of
    tickets = jax.random.randint(jax.random.fold_in(key, 2), (rows, number_of), 0, 4096) + favour
    sure = jax.random.permutation(jax.random.fold_in(key, 3), rows)[jnp.arange(number_of) % rows]
    tickets = jnp.where(jnp.arange(rows)[:, None] == sure[None, :], 1 << 14, tickets)
    score = tickets * number_of + jnp.arange(number_of)
    return lax.top_k(score.astype(jnp.int32), top)[1].astype(jnp.int32)


def scatter_about(own_key, shape, spread, bound, split=(), held_as=jnp.bfloat16):
    gain = steps_of(own_key, shape, split, -0.22, 0.18) if split else 1.0
    result = jax.random.normal(own_key, shape, jnp.float32) * spread * gain
    return jnp.minimum(jnp.maximum(result, -bound), bound).astype(held_as)


def setup_inputs(seed: int = 0, part: int = 0) -> dict:
    seeds = jax.random.split(jax.random.key(seed), 7)
    part_keys = jax.random.split(jax.random.fold_in(seeds[6], part), 7)
    tokens = scatter_about(part_keys[0], (TOKENS, D), 1.0, 6.0, ((0, 16),))
    shrink_panels = scatter_about(seeds[1], (ADAPTERS, D, R), D ** -0.5, 0.0625, ((1, 16),))
    expand_panels = scatter_about(seeds[2], (ADAPTERS, R, D), R ** -0.5, 0.75, ((2, 16),))
    adapter_scale = jnp.clip(jnp.exp(jax.random.uniform(seeds[3], (ADAPTERS,), jnp.float32, math.log(0.5), math.log(2.0))), 0.5, 2.0)
    block_adapter = picks_of(part_keys[4], NBLOCKS, ADAPTERS, 1, 512)
    shard_counts = draw_shard_counts(jax.random.fold_in(jax.random.fold_in(seeds[6], part), 71), part)
    return {"tokens": tokens, "shrink_panels": shrink_panels, "expand_panels": expand_panels, "adapter_scale": adapter_scale, "block_adapter": block_adapter, "shard_counts": shard_counts}


def reference(tokens, shrink_panels, expand_panels, adapter_scale, block_adapter, shard_counts):
    block_count = tokens.shape[0] // BLOCK
    blocked = tokens.reshape(block_count, BLOCK, D)
    adapter_ids = block_adapter[:, 0].astype(jnp.int32)

    def one_block(args):
        block_rows, adapter = args
        down_map = lax.dynamic_index_in_dim(shrink_panels, adapter, 0, keepdims=False)
        up_map = lax.dynamic_index_in_dim(expand_panels, adapter, 0, keepdims=False)
        shrunk = jnp.dot(block_rows, down_map, preferred_element_type=jnp.float32).astype(jnp.bfloat16)
        scale_value = lax.dynamic_index_in_dim(adapter_scale, adapter, 0, keepdims=False)
        return jnp.dot(shrunk, up_map, preferred_element_type=jnp.float32) * scale_value

    expanded = lax.map(one_block, (blocked, adapter_ids)).reshape(TOKENS, D)
    within = jnp.arange(TOK_DEV, dtype=jnp.int32)
    live_rows = (within[None, :] < shard_counts[:, None]).reshape(TOKENS, 1)
    return jnp.where(live_rows, expanded, 0.0).astype(jnp.bfloat16)
```

```python
import functools

import jax
import jax.numpy as jnp
from jax import lax
from jax.experimental import pallas as pl
from jax.experimental.pallas import tpu as pltpu
from jax.sharding import PartitionSpec as P

BLOCK = 64
CHUNKS = 2
SLICES = 2
MESH = pl.DeviceIdType.MESH


def kernel(
    n, groups,
    ids, scale, counts, tok_h, s_h, e_h, out_v,
    tok, ps, pe, gs, ge, fs, fe, ss, se, guest, psum, pgot, acc, shr,
    loc, st_s, st_r, fw_s, fw_r, ax_s, ax_r, fx_s, fx_r, tk_s, tk_r, pt_s, pt_r, *distant,
):
    g, me = lax.axis_index("groups"), lax.axis_index("blk")
    h, w = n // 2, n // 4
    half, pos, q, u = me // h, me % h, me // w, me % w
    adapters, rank, feats = s_h.shape
    blocks = ss.shape[2]
    thick = rank // SLICES
    share = adapters // groups
    size = share // CHUNKS
    near_inner, near_outer = 1 + half, 3 * half
    far = (2 - half, 3 - 3 * half)
    inside = half * (3 - q) + (1 - half) * q
    inner, outer = inside == 1, inside == 0
    sources, own = (s_h, e_h), (ps, pe)
    others = [
        [distant[(2 * j + p) * SLICES:(2 * j + p + 1) * SLICES] for p in range(2)]
        for j in range(2)
    ]
    sends, far_sends, slots = (gs, ge), (fs, fe), (ss, se)

    local = [
        pltpu.make_async_copy(s_h, ps, loc.at[0]),
        pltpu.make_async_copy(e_h, pe, loc.at[1]),
        pltpu.make_async_copy(tok_h, tok, loc.at[2]),
    ]
    for copy in local:
        copy.start()

    barrier = pltpu.get_barrier_semaphore()

    def greet(group, blk):
        pl.semaphore_signal(
            barrier, inc=1, device_id={"groups": group, "blk": blk}, device_id_type=MESH
        )

    for quarter in far:
        greet(g, quarter * w + u)
    for step in range(1, groups):
        greet((g + step) % groups, me)

    @pl.loop(1, h)
    def _(k):
        greet(g, half * h + (pos + k) % h)

    pl.semaphore_wait(barrier, 2 + (groups - 1) + (h - 1))

    def remote(src, dst, send_sem, recv_sem, group, blk):
        return pltpu.make_async_remote_copy(
            src_ref=src, dst_ref=dst, send_sem=send_sem, recv_sem=recv_sem,
            device_id={"groups": group, "blk": blk}, device_id_type=MESH,
        )

    def part(group, c):
        return pl.ds(group * share + c * size, size)

    def ranks(r):
        return pl.ds(r * thick, thick)

    def across(j, p, r, c):
        return remote(
            sources[p].at[part(g, c), ranks(r)], others[j][p][r].at[part(g, c)],
            st_s.at[p, r, c], st_r.at[j, p, r, c], g, far[0] * w + u,
        )

    def forward(j, p, r, c, step):
        rows = others[j][p][r].at[part(g, c)]
        sem = (j, p, r, c, step - 1)
        return remote(rows, rows, fw_s.at[sem], fw_r.at[sem], (g + step) % groups, me)

    def forwarded(j, p, r, c, step):
        rows = others[j][p][r].at[part((g - step + groups) % groups, c)]
        sem = (j, p, r, c, step - 1)
        return remote(rows, rows, fw_s.at[sem], fw_r.at[sem], (g + step) % groups, me)

    def start_across(j, p):
        for r in range(SLICES):
            for c in range(CHUNKS):
                across(j, p, r, c).start()

    def to_peer(p, d):
        return remote(
            sends[p].at[d], slots[p].at[me], ax_s.at[p, d], ax_r.at[p, me], g, half * h + d
        )

    def to_far_peer(j, p, r, d):
        owner = far[j] * w + u
        return remote(
            far_sends[p].at[j, d, r], slots[p].at[owner, r],
            fx_s.at[j, p, r, d], fx_r.at[j, p, r, u], g, half * h + d,
        )

    def from_near(p, owner):
        rows = slots[p].at[owner]
        return remote(rows, rows, ax_s.at[p, 0], ax_r.at[p, owner], g, me)

    def from_far(j, p, r, v):
        rows = slots[p].at[far[j] * w + v, r]
        return remote(rows, rows, fx_s.at[j, p, r, 0], fx_r.at[j, p, r, v], g, me)

    def near_send(p):
        local[p].wait()

        @pl.loop(1, h + 1)
        def _(k):
            d = (pos + k) % h
            for b in range(blocks):
                panel = own[p][ids[(half * h + d) * blocks + b]]
                for r in range(SLICES):
                    sends[p][d, r, b] = panel[r * thick:(r + 1) * thick]

        @pl.loop(1, h)
        def _(k):
            to_peer(p, (pos + k) % h).start()

        slots[p][me] = sends[p][pos]

    def end_at(k):
        return (near_outer - 2 * half) * w + (u + k) % w

    def side_at(k):
        return (q - 2 * half) * w + (u + k) % w

    def far_send(j, p, r):
        panel = others[j][p][r]

        def pick(d):
            for b in range(blocks):
                far_sends[p][j, d, r, b] = panel[ids[(half * h + d) * blocks + b]]

        if p == 1 or j == 1:
            @pl.loop(0, w)
            def _(k):
                pick(end_at(k))

            @pl.loop(0, w)
            def _(k):
                to_far_peer(j, p, r, end_at(k)).start()

        @pl.loop(1, w + 1)
        def _(k):
            pick(side_at(k))

        @pl.loop(1, w)
        def _(k):
            to_far_peer(j, p, r, side_at(k)).start()

        slots[p][far[j] * w + u, r] = far_sends[p][j, side_at(0), r]

    def columns(owner):
        return pl.ds(pl.multiple_of(owner * feats, feats), feats)

    def visit(k):
        v = (u + k) % w
        return remote(
            tok_h.at[:, columns(far[0] * w + v)], guest.at[u],
            tk_s.at[v], tk_r.at[u], g, near_inner * w + v,
        )

    def visited(v):
        return remote(guest.at[v], guest.at[v], tk_s.at[v], tk_r.at[v], g, me)

    def back(v):
        return remote(psum.at[v], pgot.at[u], pt_s.at[v], pt_r.at[u], g, near_outer * w + v)

    def came_back(v):
        return remote(pgot.at[v], pgot.at[v], pt_s.at[v], pt_r.at[v], g, me)

    def down(rows, panel):
        return lax.dot_general(
            rows, panel, (((1,), (1,)), ((), ())), preferred_element_type=jnp.float32
        )

    @pl.when(inner)
    def _():
        for p in range(2):
            start_across(0, p)
        for p in range(2):
            near_send(p)
        for j, p, r in [(j, p, r) for j in range(2) for p in range(2) for r in range(SLICES)]:
            for c in range(CHUNKS):
                across(j, p, r, c).wait_recv()
                for step in range(1, groups):
                    forward(j, p, r, c, step).start()
            for c in range(CHUNKS):
                for step in range(1, groups):
                    forwarded(j, p, r, c, step).wait_recv()
            far_send(j, p, r)
            if (j, p, r) == (0, 0, SLICES - 1):
                @pl.loop(0, w)
                def _(k):
                    v = (u + k) % w
                    visited(v).wait_recv()
                    for b in range(blocks):
                        rows = guest[v, b * BLOCK:(b + 1) * BLOCK, :]
                        for i in range(SLICES):
                            panel = others[0][0][i][ids[(near_outer * w + v) * blocks + b]]
                            at = (b % 2) * rank + i * thick
                            psum[v, b // 2, :, at:at + thick] = down(rows, panel)

                @pl.loop(0, w)
                def _(k):
                    back((u + k) % w).start()

    @pl.when(outer)
    def _():
        @pl.loop(0, w)
        def _(k):
            visit(k).start()

        near_send(0)
        start_across(1, 0)
        start_across(1, 1)
        near_send(1)

    local[2].wait()
    acc[...] = jnp.zeros_like(acc)
    def each(p, quarter, j, k0, use):
        @pl.loop(0, w)
        def _(k):
            v = (u - k + w) % w

            @pl.when(k >= k0)
            def _():
                if j is None:
                    from_near(p, quarter * w + v).wait_recv()
                else:
                    for r in range(SLICES):
                        from_far(j, p, r, v).wait_recv()

            use(quarter * w + v)

    def panel_of(slot, owner, b):
        return jnp.concatenate([slot[owner, r, b] for r in range(SLICES)], axis=0)

    def shrink(owner):
        for b in range(blocks):
            acc[b] += down(tok[b * BLOCK:(b + 1) * BLOCK, columns(owner)], panel_of(ss, owner, b))

    each(0, q, None, 1, shrink)

    @pl.when(inner)
    def _():
        for j in range(2):
            each(0, far[j], j, 1, shrink)
        each(0, near_outer, None, 0, shrink)

    @pl.when(outer)
    def _():
        each(0, near_inner, None, 0, shrink)

        @pl.loop(0, w)
        def _(k):
            v = (u - k + w) % w
            came_back(v).wait_recv()
            for b in range(blocks):
                at = (b % 2) * rank
                acc[b] += pgot[v, b // 2, :, at:at + rank]

        each(0, far[1], 1, 0, shrink)

    shr[...] = acc[...].astype(shr.dtype)
    count = counts[me]
    row = lax.broadcasted_iota(jnp.int32, (BLOCK, feats), 0)

    def expand(owner):
        for b in range(blocks):
            wide = jnp.dot(shr[b], panel_of(se, owner, b), preferred_element_type=jnp.float32)
            wide = wide * scale[ids[me * blocks + b]]
            live = row < count - b * BLOCK
            out_v[b * BLOCK:(b + 1) * BLOCK, columns(owner)] = jnp.where(
                live, wide, 0.0
            ).astype(out_v.dtype)

    each(1, q, None, 1, expand)

    @pl.when(inner)
    def _():
        for j in range(2):
            each(1, far[j], j, 1, expand)
        each(1, near_outer, None, 0, expand)

    @pl.when(outer)
    def _():
        each(1, near_inner, None, 0, expand)
        for j in range(2):
            each(1, far[j], j, 0, expand)

    for p in range(2):
        for r in range(SLICES):
            for c in range(CHUNKS):
                across(0, p, r, c).wait_send()

        @pl.loop(1, h)
        def _(k):
            to_peer(p, (pos + k) % h).wait_send()

    @pl.when(inner)
    def _():
        for j, p, r in [(j, p, r) for j in range(2) for p in range(2) for r in range(SLICES)]:
            for c in range(CHUNKS):
                for step in range(1, groups):
                    forward(j, p, r, c, step).wait_send()

            @pl.loop(1, w)
            def _(k):
                to_far_peer(j, p, r, side_at(k)).wait_send()

            if p == 1 or j == 1:
                @pl.loop(0, w)
                def _(k):
                    to_far_peer(j, p, r, end_at(k)).wait_send()

        @pl.loop(0, w)
        def _(k):
            back((u + k) % w).wait_send()

    @pl.when(outer)
    def _():
        @pl.loop(0, w)
        def _(k):
            visit(k).wait_send()


def body(n, groups, tokens, shrink_panels, expand_panels, adapter_scale, block_adapter, shard_counts):
    rows, width = tokens.shape
    adapters, feats, rank = shrink_panels.shape
    blocks = rows // BLOCK
    h, w = n // 2, n // 4
    bf16 = tokens.dtype
    dma = pltpu.SemaphoreType.DMA
    smem = pl.BlockSpec(memory_space=pltpu.SMEM)
    hbm = pl.BlockSpec(memory_space=pl.ANY)
    panel = pltpu.VMEM((adapters, rank, feats), bf16)
    slice_of = pltpu.VMEM((adapters, rank // SLICES, feats), bf16)
    moved = (SLICES, blocks, rank // SLICES, feats)
    near = pltpu.VMEM((h, *moved), bf16)
    distant = pltpu.VMEM((2, h, *moved), bf16)
    slot = pltpu.VMEM((n, *moved), bf16)
    sums = pltpu.VMEM((w, (blocks + 1) // 2, BLOCK, 2 * rank), jnp.float32)
    return pl.pallas_call(
        functools.partial(kernel, n, groups),
        out_shape=pltpu.VMEM((rows, width), bf16),
        in_specs=[smem, smem, smem, hbm, hbm, hbm],
        out_specs=pl.BlockSpec(memory_space=pltpu.VMEM),
        scratch_shapes=[
            pltpu.VMEM((rows, width), bf16),
            panel, panel,
            near, near, distant, distant, slot, slot,
            pltpu.VMEM((w, rows, feats), bf16),
            sums, sums,
            pltpu.VMEM((blocks, BLOCK, rank), jnp.float32),
            pltpu.VMEM((blocks, BLOCK, rank), bf16),
            dma((3,)),
            dma((2, SLICES, CHUNKS)), dma((2, 2, SLICES, CHUNKS)),
            dma((2, 2, SLICES, CHUNKS, groups - 1)), dma((2, 2, SLICES, CHUNKS, groups - 1)),
            dma((2, h)), dma((2, n)), dma((2, 2, SLICES, h)), dma((2, 2, SLICES, w)),
            dma((w,)), dma((w,)), dma((w,)), dma((w,)),
            *[slice_of] * (4 * SLICES),
        ],
        compiler_params=pltpu.CompilerParams(
            collective_id=0, has_side_effects=True, vmem_limit_bytes=56 * 1024 * 1024
        ),
    )(
        block_adapter[:, 0], adapter_scale, shard_counts,
        tokens, jnp.swapaxes(shrink_panels, 1, 2), expand_panels,
    )


def solution(mesh):
    return jax.shard_map(
        functools.partial(body, mesh.shape["blk"], mesh.shape["groups"]),
        mesh=mesh,
        in_specs=(
            P(("groups", "blk"), None),
            P(None, "blk", None),
            P(None, None, "blk"),
            P(),
            P("groups", None),
            P("groups"),
        ),
        out_specs=P(("groups", "blk"), None),
        check_vma=False,
    )
```

```python
import functools

import jax
import jax.numpy as jnp
from jax import lax
from jax.experimental import pallas as pl
from jax.experimental.pallas import tpu as pltpu
from jax.sharding import PartitionSpec as P

BLOCK = 64
UNIT = 16
MESH = pl.DeviceIdType.MESH


def kernel(
    n, groups,
    ids, scale, counts, ids_h, tok_h, s_h, e_h, out_v,
    tok, ps, pe, ns, ne, fs, far_out, rel_out, ss, se, guest, tokrel, psum, pgot, acc, shr, idx_v, idx_s,
    loc, id_s, id_r, id_c, ns_s, ne_s, fs_s, fo_s, ro_s, sl_r,
    rl_s, rl_r, ac_s, ac_r, fw_s, fw_r, xs_s, xs_r,
    ty_s, ty_r, tk_s, tk_r, pt_s, pt_r, *held,
):
    g, me = lax.axis_index("groups"), lax.axis_index("blk")
    h, w = n // 2, n // 4
    half, q, u = me // h, me // w, me % w
    adapters, rank, feats = s_h.shape
    blocks = ss.shape[2]
    units = rank // UNIT
    per = units // groups
    near_inner, near_outer = 1 + half, 3 * half
    far_inner, far_outer = 2 - half, 3 - 3 * half
    inside = half * (3 - q) + (1 - half) * q
    inner, outer = inside == 1, inside == 0
    side = w // 2
    mate = (u + side) % w
    row_of = u // side
    sources, own, slots = (s_h, e_h), (ps, pe), (ss, se)
    far_s = held[:units]
    rest = held[units:]
    far_e, end_s, end_e, rel_s, rel_e = [rest[i * per:(i + 1) * per] for i in range(5)]
    ends, rels = (end_s, end_e), (rel_s, rel_e)

    local = [
        pltpu.make_async_copy(s_h, ps, loc.at[0]),
        pltpu.make_async_copy(e_h, pe, loc.at[1]),
        pltpu.make_async_copy(tok_h, tok, loc.at[2]),
    ]
    for copy in (local[1], local[0], local[2]):
        copy.start()

    barrier = pltpu.get_barrier_semaphore()

    def greet(group, blk):
        pl.semaphore_signal(
            barrier, inc=1, device_id={"groups": group, "blk": blk}, device_id_type=MESH
        )

    @pl.loop(1, groups * h)
    def _(k):
        greet((g + k // h) % groups, half * h + (me + k) % h)

    @pl.when(inner)
    def _():
        greet(g, far_inner * w + u)

    pl.semaphore_wait(barrier, groups * h - 1 + jnp.where(inner, 1, 0))

    def remote(src, dst, send_sem, recv_sem, group, blk):
        return pltpu.make_async_remote_copy(
            src_ref=src, dst_ref=dst, send_sem=send_sem, recv_sem=recv_sem,
            device_id={"groups": group, "blk": blk}, device_id_type=MESH,
        )

    def unit_of(group, s):
        return group * per + s

    def mine(p, s):
        return sources[p].at[:, pl.ds(pl.multiple_of(unit_of(g, s) * UNIT, UNIT), UNIT)]

    def columns(owner, count=1):
        return pl.ds(pl.multiple_of(owner * feats, feats), count * feats)

    def id_of(step, blk, b):
        if step == 0:
            return ids[blk * blocks + b]
        return idx_s[(g + step) % groups, 0, blk * blocks + b]

    def ids_copy(step):
        return remote(
            ids_h, idx_v.at[g], id_s.at[step - 1], id_r.at[g], (g + step) % groups, me
        )

    def ids_got(step):
        rows = idx_v.at[(g - step + groups) % groups]
        return remote(rows, rows, id_s.at[step - 1], id_r.at[(g - step + groups) % groups], g, me)

    def relay(p, s):
        return remote(
            mine(p, s), rels[p][s], rl_s.at[p, s], rl_r.at[p, s], g, near_inner * w + u
        )

    def across(p, s):
        if p == 1:
            return remote(
                mine(1, s), far_e[s], ac_s.at[1, s], ac_r.at[1, s], g, far_inner * w + u
            )
        raise NotImplementedError

    def forward(p, s):
        return remote(
            rels[p][s], ends[p][s], fw_s.at[p, s], fw_r.at[p, s], g, far_inner * w + u
        )

    def near_copy(p, plane, v):
        buf, sem = ((ns, ns_s), (ne, ne_s))[p]
        at = jnp.where(plane == q, 0, w) + v if p else v
        return remote(
            buf.at[at], slots[p].at[me], sem.at[at], sl_r.at[p, me, 0], g, plane * w + v
        )

    def near_fill(p, plane, v, at):
        buf = (ns, ne)[p]
        for b in range(blocks):
            panel = own[p][id_of(0, plane * w + v, b)]
            for un in range(units):
                buf[at, un, b] = panel[un * UNIT:(un + 1) * UNIT]

    def near_own(p):
        @pl.loop(0, w)
        def _(k):
            v = (u + k) % w
            near_fill(p, q, v, v)

        @pl.loop(1, w)
        def _(k):
            near_copy(p, q, (u + k) % w).start()

        slots[p][me] = (ns, ne)[p][u]

    def near_end():
        @pl.loop(0, w)
        def _(k):
            v = (u + k) % w
            near_fill(1, near_outer, v, w + v)

        @pl.loop(0, w)
        def _(k):
            near_copy(1, near_outer, (u + k) % w).start()

    def part_copy(p, owner, un, buf, sem, step, plane, i, v):
        return remote(
            buf.at[step, i * w + v], slots[p].at[owner, un], sem.at[step, i * w + v],
            sl_r.at[p, owner, un], (g + step) % groups, plane * w + v,
        )

    def part_send(p, src, s, quarter, buf, sem, planes):
        owner, un = quarter * w + u, unit_of(g, s)
        for i, plane in enumerate(planes):
            last = i == len(planes) - 1
            for step in range(groups):
                @pl.loop(0, w)
                def _(k, step=step, plane=plane, i=i):
                    v = (u + k) % w
                    for b in range(blocks):
                        buf[step, i * w + v, b] = src[id_of(step, plane * w + v, b)]

                @pl.loop(1 if last and step == 0 else 0, w)
                def _(k, step=step, plane=plane, i=i):
                    part_copy(p, owner, un, buf, sem, step, plane, i, (u + k) % w).start()

        slots[p][owner, un] = buf[0, (len(planes) - 1) * w + u]

    def part_done(p, s, quarter, buf, sem, planes):
        owner, un = quarter * w + u, unit_of(g, s)
        for i, plane in enumerate(planes):
            last = i == len(planes) - 1
            for step in range(groups):
                @pl.loop(1 if last and step == 0 else 0, w)
                def _(k, step=step, plane=plane, i=i):
                    part_copy(p, owner, un, buf, sem, step, plane, i, (u + k) % w).wait_send()

    def part_got(p, owner, un):
        rows = slots[p].at[owner, un]
        return remote(rows, rows, sl_s_dummy(), sl_r.at[p, owner, un], g, me)

    def sl_s_dummy():
        return loc.at[3]

    def full_got(p, owner):
        rows = slots[p].at[owner]
        return remote(rows, rows, sl_s_dummy(), sl_r.at[p, owner, 0], g, me)

    def cross_s(step, s):
        un = unit_of(g, s)
        return [
            (un == i, remote(
                s_h.at[:, pl.ds(i * UNIT, UNIT)], far_s[i], ac_s.at[0, s], ac_r.at[0, i],
                g, far_inner * w + u,
            )) for i in range(units)
        ]

    def start_cross_s(s):
        for chosen, copy in cross_s(0, s):
            @pl.when(chosen)
            def _(copy=copy):
                copy.start()

    def share_s(i, step):
        return remote(
            far_s[i], far_s[i], xs_s.at[i, step - 1], xs_r.at[i], (g + step) % groups, me
        )

    def take_s(s):
        un = unit_of(g, s)
        for i in range(units):
            @pl.when(un == i)
            def _(i=i):
                remote(far_s[i], far_s[i], ac_s.at[0, s], ac_r.at[0, i], g, me).wait_recv()
                for step in range(1, groups):
                    share_s(i, step).start()

    def shared_s():
        for i in range(units):
            @pl.when(i // per != g)
            def _(i=i):
                remote(far_s[i], far_s[i], xs_s.at[i, 0], xs_r.at[i], g, me).wait_recv()

    def far_copy(v):
        return remote(
            fs.at[v], ss.at[far_inner * w + u], fs_s.at[v], sl_r.at[0, far_inner * w + u, 0],
            g, near_inner * w + v,
        )

    def far_own():
        @pl.loop(0, w)
        def _(k):
            v = (u + k) % w
            for b in range(blocks):
                a = id_of(0, near_inner * w + v, b)
                for i in range(units):
                    fs[v, i, b] = far_s[i][a]

        @pl.loop(1, w)
        def _(k):
            far_copy((u + k) % w).start()

        ss[far_inner * w + u] = fs[u]

    def visit_quarter(f):
        return (near_inner, far_inner)[f]

    def pass_rows(f):
        return remote(
            tok_h.at[:, columns(visit_quarter(f) * w + (mate // side) * side, side)],
            tokrel.at[f], ty_s.at[f], ty_r.at[f], g, near_outer * w + mate,
        )

    def visit(f, i):
        v = row_of * side + i
        return remote(
            tok_h.at[:, columns(visit_quarter(f) * w + v)], guest.at[f, u],
            tk_s.at[f, 0, i], tk_r.at[f, u], g, near_inner * w + v,
        )

    def visit_mate(f, i):
        v = row_of * side + i
        return remote(
            tokrel.at[f, :, pl.ds(i * feats, feats)], guest.at[f, mate],
            tk_s.at[f, 1, i], tk_r.at[f, mate], g, near_inner * w + v,
        )

    def visited(f, v):
        return remote(guest.at[f, v], guest.at[f, v], sl_s_dummy(), tk_r.at[f, v], g, me)

    def back(v):
        return remote(psum.at[v], pgot.at[u], pt_s.at[v], pt_r.at[u], g, near_outer * w + v)

    def came_back(v):
        return remote(pgot.at[v], pgot.at[v], sl_s_dummy(), pt_r.at[v], g, me)

    def down(rows, panel):
        return lax.dot_general(
            rows, panel, (((1,), (1,)), ((), ())), preferred_element_type=jnp.float32
        )

    def host(f):
        @pl.loop(0, w)
        def _(k):
            v = (u + k) % w
            visited(f, v).wait_recv()
            for b in range(blocks):
                rows = guest[f, v, b * BLOCK:(b + 1) * BLOCK, :]
                a = id_of(0, near_outer * w + v, b)
                if f == 0:
                    panel = ps[a]
                else:
                    panel = jnp.concatenate([far_s[i][a] for i in range(units)], axis=0)
                at = (b % 2) * rank
                part = down(rows, panel)
                if f == 0:
                    psum[v, b // 2, :, at:at + rank] = part
                else:
                    psum[v, b // 2, :, at:at + rank] += part

    def panel_of(slot, owner, b):
        return jnp.concatenate([slot[owner, i, b] for i in range(units)], axis=0)

    def shrink(owner):
        for b in range(blocks):
            acc[b] += down(tok[b * BLOCK:(b + 1) * BLOCK, columns(owner)], panel_of(ss, owner, b))

    count = counts[me]
    row = lax.broadcasted_iota(jnp.int32, (BLOCK, feats), 0)

    def expand(owner):
        for b in range(blocks):
            wide = jnp.dot(shr[b], panel_of(se, owner, b), preferred_element_type=jnp.float32)
            wide = wide * scale[ids[me * blocks + b]]
            live = row < count - b * BLOCK
            out_v[b * BLOCK:(b + 1) * BLOCK, columns(owner)] = jnp.where(
                live, wide, 0.0
            ).astype(out_v.dtype)

    def each_full(p, quarter, k0, use):
        @pl.loop(0, w)
        def _(k):
            v = (u - k + w) % w

            @pl.when(k >= k0)
            def _():
                full_got(p, quarter * w + v).wait_recv()

            use(quarter * w + v)

    def each_part(p, quarter, k0, use):
        @pl.loop(0, w)
        def _(k):
            v = (u - k + w) % w
            for step in range(groups):
                for s in range(per):
                    un = unit_of((g + step) % groups, s)
                    if step == 0:
                        @pl.when(k >= k0)
                        def _(un=un):
                            part_got(p, quarter * w + v, un).wait_recv()
                    else:
                        part_got(p, quarter * w + v, un).wait_recv()
            use(quarter * w + v)

    both, near = (near_outer, near_inner), (near_inner,)

    def take_end(p, s):
        forward_got = remote(ends[p][s], ends[p][s], fw_s.at[p, s], fw_r.at[p, s], g, me)
        forward_got.wait_recv()
        part_send(p, ends[p][s], s, far_outer, far_out.at[1 + p, s], fo_s.at[1 + p, s], both)

    def take_far_e(s):
        remote(far_e[s], far_e[s], ac_s.at[1, s], ac_r.at[1, s], g, me).wait_recv()
        part_send(1, far_e[s], s, far_inner, far_out.at[0, s], fo_s.at[0, s], both)

    def take_relay(p, s):
        remote(rels[p][s], rels[p][s], rl_s.at[p, s], rl_r.at[p, s], g, me).wait_recv()
        forward(p, s).start()
        part_send(p, rels[p][s], s, near_outer, rel_out.at[p, s], ro_s.at[p, s], near)

    @pl.when(inner)
    def _():
        for step in range(1, groups):
            ids_copy(step).start()
        for s in range(per):
            across(1, s).start()
        local[1].wait()
        near_end()
        near_own(1)
        local[0].wait()
        near_own(0)
        for step in range(1, groups):
            other = (g - step + groups) % groups
            ids_got(step).wait_recv()
            copy = pltpu.make_async_copy(idx_v.at[other], idx_s.at[other], id_c.at[step - 1])
            copy.start()
            copy.wait()
        for s in range(per):
            take_relay(0, s)
            take_far_e(s)
        for s in range(per - 1):
            start_cross_s(s)
        for s in range(per):
            take_end(0, s)
        host(0)
        local[2].wait()
        acc[...] = jnp.zeros_like(acc)
        each_full(0, q, 1, shrink)
        each_part(0, near_outer, 1, shrink)
        for s in range(per):
            if s == per - 1:
                start_cross_s(s)
            take_relay(1, s)
        for s in range(per - 1):
            take_s(s)
            take_end(1, s)
        each_part(0, far_outer, 1, shrink)
        take_s(per - 1)
        shared_s()
        far_own()
        host(1)

        @pl.loop(0, w)
        def _(k):
            back((u + k) % w).start()

        take_end(1, per - 1)
        each_full(0, far_inner, 1, shrink)
        shr[...] = acc[...].astype(shr.dtype)
        each_full(1, q, 1, expand)
        each_part(1, far_inner, 1, expand)
        each_part(1, near_outer, 1, expand)
        each_part(1, far_outer, 1, expand)

        for step in range(1, groups):
            ids_copy(step).wait_send()
        for s in range(per):
            across(1, s).wait_send()
            for chosen, copy in cross_s(0, s):
                @pl.when(chosen)
                def _(copy=copy):
                    copy.wait_send()
            part_done(1, s, far_inner, far_out.at[0, s], fo_s.at[0, s], both)
            for p in range(2):
                forward(p, s).wait_send()
                part_done(p, s, far_outer, far_out.at[1 + p, s], fo_s.at[1 + p, s], both)
                part_done(p, s, near_outer, rel_out.at[p, s], ro_s.at[p, s], near)
        for i in range(units):
            @pl.when(i // per == g)
            def _(i=i):
                for step in range(1, groups):
                    share_s(i, step).wait_send()

        @pl.loop(1, w)
        def _(k):
            far_copy((u + k) % w).wait_send()

        @pl.loop(0, w)
        def _(k):
            near_copy(1, near_outer, (u + k) % w).wait_send()
            back((u + k) % w).wait_send()

    @pl.when(outer)
    def _():
        for s in range(per):
            relay(0, s).start()
        pass_rows(0).start()
        for i in range(side):
            visit(0, i).start()
        local[0].wait()
        near_own(0)
        pass_rows(1).start()
        local[1].wait()
        near_own(1)

        def rows_got(f):
            remote(tokrel.at[f], tokrel.at[f], ty_s.at[f], ty_r.at[f], g, me).wait_recv()

        rows_got(0)
        for i in range(side):
            visit_mate(0, i).start()
        for s in range(per):
            relay(1, s).start()
        for i in range(side):
            visit(1, i).start()
        rows_got(1)
        for i in range(side):
            visit_mate(1, i).start()
        local[2].wait()
        acc[...] = jnp.zeros_like(acc)
        each_full(0, q, 1, shrink)
        each_part(0, far_outer, 0, shrink)

        @pl.loop(0, w)
        def _(k):
            v = (u - k + w) % w
            came_back(v).wait_recv()
            for b in range(blocks):
                at = (b % 2) * rank
                acc[b] += pgot[v, b // 2, :, at:at + rank]

        shr[...] = acc[...].astype(shr.dtype)
        each_full(1, q, 1, expand)
        each_full(1, near_inner, 0, expand)
        each_part(1, far_inner, 0, expand)
        each_part(1, far_outer, 0, expand)

        for f in range(2):
            pass_rows(f).wait_send()
            for i in range(side):
                visit(f, i).wait_send()
                visit_mate(f, i).wait_send()
        for p in range(2):
            for s in range(per):
                relay(p, s).wait_send()

    for p in range(2):
        @pl.loop(1, w)
        def _(k, p=p):
            near_copy(p, q, (u + k) % w).wait_send()


def body(n, groups, tokens, shrink_panels, expand_panels, adapter_scale, block_adapter, shard_counts):
    rows, width = tokens.shape
    adapters, feats, rank = shrink_panels.shape
    blocks = rows // BLOCK
    h, w = n // 2, n // 4
    units = rank // UNIT
    per = units // groups
    side = w // 2
    bf16 = tokens.dtype
    dma = pltpu.SemaphoreType.DMA
    smem = pl.BlockSpec(memory_space=pltpu.SMEM)
    hbm = pl.BlockSpec(memory_space=pl.ANY)
    panel = pltpu.VMEM((adapters, rank, feats), bf16)
    moved = (units, blocks, UNIT, feats)
    one = (blocks, UNIT, feats)
    slot = pltpu.VMEM((n, *moved), bf16)
    sums = pltpu.VMEM((w, (blocks + 1) // 2, BLOCK, 2 * rank), jnp.float32)
    ids = jnp.swapaxes(block_adapter, 0, 1)
    return pl.pallas_call(
        functools.partial(kernel, n, groups),
        out_shape=pltpu.VMEM((rows, width), bf16),
        in_specs=[smem, smem, smem, hbm, hbm, hbm, hbm],
        out_specs=pl.BlockSpec(memory_space=pltpu.VMEM),
        scratch_shapes=[
            pltpu.VMEM((rows, width), bf16),
            panel, panel,
            pltpu.VMEM((w, *moved), bf16),
            pltpu.VMEM((2 * w, *moved), bf16),
            pltpu.VMEM((w, *moved), bf16),
            pltpu.VMEM((3, per, groups, h, *one), bf16),
            pltpu.VMEM((2, per, groups, w, *one), bf16),
            slot, slot,
            pltpu.VMEM((2, w, rows, feats), bf16),
            pltpu.VMEM((2, rows, side * feats), bf16),
            sums, sums,
            pltpu.VMEM((blocks, BLOCK, rank), jnp.float32),
            pltpu.VMEM((blocks, BLOCK, rank), bf16),
            pltpu.VMEM((groups, 1, n * blocks), jnp.int32),
            pltpu.SMEM((groups, 1, n * blocks), jnp.int32),
            dma((4,)), dma((groups,)), dma((groups,)), dma((groups,)),
            dma((w,)), dma((2 * w,)), dma((w,)),
            dma((3, per, groups, h)), dma((2, per, groups, w)), dma((2, n, units)),
            dma((2, per)), dma((2, per)), dma((2, per)), dma((2, units)),
            dma((2, per)), dma((2, per)), dma((units, groups)), dma((units,)),
            dma((2,)), dma((2,)), dma((2, 2, side)), dma((2, w)), dma((w,)), dma((w,)),
            *[pltpu.VMEM((adapters, UNIT, feats), bf16)] * (units + 5 * per),
        ],
        compiler_params=pltpu.CompilerParams(
            collective_id=0, has_side_effects=True, vmem_limit_bytes=56 * 1024 * 1024
        ),
    )(
        block_adapter[:, 0], adapter_scale, shard_counts, ids,
        tokens, jnp.swapaxes(shrink_panels, 1, 2), expand_panels,
    )


def solution(mesh):
    return jax.shard_map(
        functools.partial(body, mesh.shape["blk"], mesh.shape["groups"]),
        mesh=mesh,
        in_specs=(
            P(("groups", "blk"), None),
            P(None, "blk", None),
            P(None, None, "blk"),
            P(),
            P("groups", None),
            P("groups"),
        ),
        out_specs=P(("groups", "blk"), None),
        check_vma=False,
    )
```
